32 devices in a mesh: fsdp: 8 (over y, x, core), tp: 4 (over z).
Axes of the slice: x: 2, y: 2, z: 4, core: 2. Of those that a mesh axis runs over, the one named last changes fastest.
Arguments:
- tokens: bfloat16 [16, 1376, 1024], P('fsdp', 'tp'), may hold values from -6 to 6
- w_query: bfloat16 [1024, 1024], P('fsdp', 'tp'), may hold values from -0.375 to 0.375
- w_key: bfloat16 [1024, 1024], P('fsdp', 'tp'), may hold values from -0.1875 to 0.1875
- w_value: bfloat16 [1024, 1024], P('fsdp', 'tp'), may hold values from -0.1875 to 0.1875
- w_out: bfloat16 [1024, 1024], P('tp', 'fsdp'), may hold values from -1 to 1
- w_up: bfloat16 [1024, 4096], P('fsdp', 'tp'), may hold values from -0.1875 to 0.1875
- w_down: bfloat16 [4096, 1024], P('tp', 'fsdp'), may hold values from -0.09375 to 0.09375
- norm1_gain: float32 [1024], replicated, may hold values from 0.5 to 1.5
- norm1_bias: float32 [1024], replicated, may hold values from -1.75 to 1.75
- query_bias: float32 [1024], replicated, may hold values from -3 to 3
- value_bias: float32 [1024], replicated, may hold values from -3 to 3
- out_bias: float32 [1024], replicated, may hold values from -1.75 to 1.75
- scale1: float32 [1024], replicated, may hold values from 0.5 to 1.5
- norm2_gain: float32 [1024], replicated, may hold values from 0.5 to 1.5
- norm2_bias: float32 [1024], replicated, may hold values from -1.75 to 1.75
- up_bias: float32 [4096], replicated, may hold values from -3 to 3
- down_bias: float32 [1024], replicated, may hold values from -1.75 to 1.75
- scale2: float32 [1024], replicated, may hold values from 0.5 to 1.5
- out_grad: bfloat16 [16, 1376, 1024], P('fsdp', 'tp'), may hold values from -6 to 6
Outputs:
- output: bfloat16 [16, 1376, 1024], P('fsdp', 'tp')
- tokens_grad: float32 [16, 1376, 1024], P('fsdp', 'tp')
- w_query_grad: float32 [1024, 1024], P('fsdp', 'tp')
- w_key_grad: float32 [1024, 1024], P('fsdp', 'tp')
- w_value_grad: float32 [1024, 1024], P('fsdp', 'tp')
- w_out_grad: float32 [1024, 1024], P('tp', 'fsdp')
- w_up_grad: float32 [1024, 4096], P('fsdp', 'tp')
- w_down_grad: float32 [4096, 1024], P('tp', 'fsdp')
- norm1_gain_grad: float32 [1024], replicated
- norm1_bias_grad: float32 [1024], replicated
- query_bias_grad: float32 [1024], replicated
- value_bias_grad: float32 [1024], replicated
- out_bias_grad: float32 [1024], replicated
- scale1_grad: float32 [1024], replicated
- norm2_gain_grad: float32 [1024], replicated
- norm2_bias_grad: float32 [1024], replicated
- up_bias_grad: float32 [4096], replicated
- down_bias_grad: float32 [1024], replicated
- scale2_grad: float32 [1024], replicated
The draws below stay inside these ranges and needn't reach their ends.
All inputs are finite; a program needn't handle non-finite values.
Results may differ from the reference program's by a relative error of at most 0.02.
Values may be sent and summed in bfloat16 or wider, within the bound.
A program may use at most 256 MiB of HBM per device.

```python
import jax
import jax.numpy as jnp
from jax import lax

D = 1024
H = 16
HD = 64
FF = 4096
SEQ = 1370
IMG_DEV = 2
Q_SPLIT = 2
SEQ_PAD = 1376
IMAGES = 16


def levels(key, dims, cuts, least, top_value):
    def one(position, parts):
        heights = jax.random.uniform(jax.random.fold_in(jax.random.fold_in(key, 6), position), (parts,), jnp.float32, least / len(cuts), top_value / len(cuts))
        return jnp.repeat(jnp.exp(heights), dims[position] // parts).reshape((-1,) + (1,) * (len(dims) - position - 1))

    gain = one(*cuts[0])
    for cut in cuts[1:]:
        gain = gain * one(*cut)
    return gain


def centred(rng, extent, scale, limit, shards=(), dtype=jnp.bfloat16):
    drawn = jax.random.normal(rng, extent, jnp.float32) * scale
    if len(shards) > 0:
        drawn = levels(rng, extent, shards, -0.22, 0.18) * drawn
    return jnp.clip(drawn, min=-limit, max=limit).astype(dtype)


def setup_inputs(seed: int = 0) -> dict:
    seeds = jax.random.split(jax.random.key(seed), 20)
    return {
        "tokens": centred(seeds[0], (IMAGES, SEQ_PAD, D), 1.0, 6.0, ((0, 8), (1, 4))),
        "w_query": centred(seeds[1], (D, D), (D // 4) ** -0.5, 0.375, ((0, 8), (1, 4))),
        "w_key": centred(seeds[2], (D, D), D ** -0.5, 0.1875, ((0, 8), (1, 4))),
        "w_value": centred(seeds[3], (D, D), D ** -0.5, 0.1875, ((0, 8), (1, 4))),
        "w_out": centred(seeds[4], (D, D), (D // 32) ** -0.5, 1.0, ((0, 4), (1, 8))),
        "w_up": centred(seeds[5], (D, FF), D ** -0.5, 0.1875, ((0, 8), (1, 4))),
        "w_down": centred(seeds[6], (FF, D), FF ** -0.5, 0.09375, ((0, 4), (1, 8))),
        "norm1_gain": jnp.clip(1.0 + 0.1 * jax.random.normal(seeds[7], (D,), jnp.float32), 0.5, 1.5),
        "norm1_bias": centred(seeds[8], (D,), 0.3, 1.75, (), jnp.float32),
        "query_bias": centred(seeds[9], (D,), 0.5, 3.0, (), jnp.float32),
        "value_bias": centred(seeds[10], (D,), 0.5, 3.0, (), jnp.float32),
        "out_bias": centred(seeds[11], (D,), 0.3, 1.75, (), jnp.float32),
        "scale1": jnp.clip(jax.random.uniform(seeds[12], (D,), jnp.float32, 0.5, 1.5), 0.5, 1.5),
        "norm2_gain": jnp.clip(1.0 + 0.1 * jax.random.normal(seeds[13], (D,), jnp.float32), 0.5, 1.5),
        "norm2_bias": centred(seeds[14], (D,), 0.3, 1.75, (), jnp.float32),
        "up_bias": centred(seeds[15], (FF,), 0.5, 3.0, (), jnp.float32),
        "down_bias": centred(seeds[16], (D,), 0.3, 1.75, (), jnp.float32),
        "scale2": jnp.clip(jax.random.uniform(seeds[17], (D,), jnp.float32, 0.5, 1.5), 0.5, 1.5),
        "out_grad": centred(seeds[18], (IMAGES, SEQ_PAD, D), 1.0, 6.0, ((0, 8), (1, 4))),
    }


@jax.custom_vjp
def low(v):
    return lax.optimization_barrier(v.astype(jnp.bfloat16)).astype(jnp.float32)

@jax.custom_vjp
def low_back(v):
    return v

def low_keep(v):
    return (low(v), None)

def low_pass(kept, grad):
    return (grad,)

def back_keep(v):
    return (v, None)

def back_low(kept, grad):
    return (low(grad),)
low.defvjp(low_keep, low_pass)
low_back.defvjp(back_keep, back_low)

def layer_norm(values, norm_gain, norm_bias):
    center = values - lax.optimization_barrier(jnp.mean(values, axis=-1, keepdims=True))
    spread = lax.optimization_barrier(jnp.mean(center * center, axis=-1, keepdims=True))
    return center * lax.rsqrt(spread + 1e-06) * norm_gain + norm_bias

def attend(queries, keys_all, values):
    highest = lax.Precision.HIGHEST
    key_valid = jnp.arange(SEQ_PAD) < SEQ
    block_rows = SEQ_PAD // Q_SPLIT

    def one_block(block_q):
        scores = low_back(jnp.einsum('hqd,hkd->hqk', block_q, keys_all, precision=highest) * 0.125)
        scores = jnp.where(key_valid, scores, -1e+30)
        largest = lax.optimization_barrier(jnp.max(scores, axis=-1, keepdims=True))
        expo = jnp.exp(scores - largest)
        shares = low(expo / lax.optimization_barrier(jnp.sum(expo, axis=-1, keepdims=True)))
        return jnp.einsum('hqk,hkd->hqd', shares, values, precision=highest)
    blocks_q = queries.reshape(H, Q_SPLIT, block_rows, HD).transpose(1, 0, 2, 3)
    result = lax.map(jax.checkpoint(one_block), blocks_q)
    return result.transpose(1, 0, 2, 3).reshape(H, SEQ_PAD, HD)

def forward(group, params):
    w_query, w_key, w_value, w_out, w_up, w_down, norm1_gain, norm1_bias, query_bias, value_bias, out_bias, scale1, norm2_gain, norm2_bias, up_bias, down_bias, scale2 = params
    highest = lax.Precision.HIGHEST
    rows_all = group.reshape(IMG_DEV * SEQ_PAD, D)
    normed = low(layer_norm(rows_all, norm1_gain, norm1_bias))
    queries = low(low_back(jnp.dot(normed, w_query, precision=highest)) + query_bias)
    keys_all = low(low_back(jnp.dot(normed, w_key, precision=highest)))
    values = low(low_back(jnp.dot(normed, w_value, precision=highest)) + value_bias)

    def split_heads(matrix):
        return matrix.reshape(IMG_DEV, SEQ_PAD, H, HD).transpose(0, 2, 1, 3)

    def attend_tuple(triple):
        return attend(triple[0], triple[1], triple[2])
    attended = lax.map(attend_tuple, (split_heads(queries), split_heads(keys_all), split_heads(values)))
    attended = attended.transpose(0, 2, 1, 3).reshape(IMG_DEV * SEQ_PAD, D)
    attended = low(low_back(attended))
    branch = low_back(jnp.dot(attended, w_out, precision=highest)) + out_bias
    middle = rows_all + scale1 * branch
    normed2 = low(layer_norm(middle, norm2_gain, norm2_bias))
    preact = low_back(jnp.dot(normed2, w_up, precision=highest)) + up_bias
    hidden = low(jax.nn.gelu(preact, approximate=False))
    feed = low_back(jnp.dot(hidden, w_down, precision=highest)) + down_bias
    final = middle + scale2 * feed
    valid = (jnp.arange(SEQ_PAD) < SEQ).astype(jnp.float32)
    return final.reshape(IMG_DEV, SEQ_PAD, D) * valid[None, :, None]

def reference(tokens, w_query, w_key, w_value, w_out, w_up, w_down, norm1_gain, norm1_bias, query_bias, value_bias, out_bias, scale1, norm2_gain, norm2_bias, up_bias, down_bias, scale2, out_grad):
    params = tuple((item.astype(jnp.float32) for item in (w_query, w_key, w_value, w_out, w_up, w_down, norm1_gain, norm1_bias, query_bias, value_bias, out_bias, scale1, norm2_gain, norm2_bias, up_bias, down_bias, scale2)))
    groups = IMAGES // IMG_DEV
    inputs = tokens.astype(jnp.float32).reshape(groups, IMG_DEV, SEQ_PAD, D)
    cotangents = out_grad.astype(jnp.float32).reshape(groups, IMG_DEV, SEQ_PAD, D)

    def one_group(totals, pair):
        result, backward = jax.vjp(forward, pair[0], params)
        input_grad, param_grads = backward(pair[1])
        totals = tuple((total + grad for total, grad in zip(totals, param_grads)))
        return (totals, (result, input_grad))
    start = tuple((jnp.zeros_like(item) for item in params))
    totals, (results, input_grads) = lax.scan(one_group, start, (inputs, cotangents))
    output = results.reshape(IMAGES, SEQ_PAD, D).astype(jnp.bfloat16)
    tokens_grad = input_grads.reshape(IMAGES, SEQ_PAD, D)
    return (output, tokens_grad, totals[0], totals[1], totals[2], totals[3], totals[4], totals[5], totals[6], totals[7], totals[8], totals[9], totals[10], totals[11], totals[12], totals[13], totals[14], totals[15], totals[16])
```

```python
import functools
import math

import jax
import jax.numpy as jnp
from jax import lax
from jax.experimental import pallas as pl
from jax.experimental.pallas import tpu as pltpu
from jax.sharding import PartitionSpec as P

HD = 64
SEQ = 1370
Q_SPLIT = 2
LANES = 128
NEG = -1e30

norm_epsilon = 1e-06


def layer_norm_parts(values):
    center = values - jnp.mean(values, axis=-1, keepdims=True)
    spread = jnp.mean(center * center, axis=-1, keepdims=True)
    inverse = lax.rsqrt(spread + norm_epsilon)
    return center * inverse, inverse


def layer_norm_back(cotangent, xhat, inverse, norm_gain):
    scaled = cotangent * norm_gain
    first = jnp.mean(scaled, axis=-1, keepdims=True)
    second = jnp.mean(scaled * xhat, axis=-1, keepdims=True)
    return (
        inverse * (scaled - first - xhat * second),
        jnp.sum(cotangent * xhat, axis=tuple(range(cotangent.ndim - 1))),
        jnp.sum(cotangent, axis=tuple(range(cotangent.ndim - 1))),
    )


def dot(left, right, left_dim, right_dim):
    return lax.dot_general(
        left,
        right,
        (((left_dim,), (right_dim,)), ((), ())),
        preferred_element_type=jnp.float32,
    )


def head_operands(queries, keys, head):
    lane_q = lax.broadcasted_iota(jnp.int32, queries.shape, 1)
    lane_k = lax.broadcasted_iota(jnp.int32, keys.shape, 1)
    row_k = lax.broadcasted_iota(jnp.int32, keys.shape, 0)
    spare = (1 - head) * HD
    own_q = (lane_q >= head * HD) & (lane_q < (head + 1) * HD)
    scaled = queries.astype(jnp.float32) * 0.125
    query_plain = jnp.where(own_q, scaled, 0.0)
    query_mask = jnp.where(lane_q == spare, 1.0, query_plain)
    key_mask = jnp.where(
        lane_k == spare, jnp.where(row_k < SEQ, 0.0, NEG), keys.astype(jnp.float32)
    )
    return (
        query_plain.astype(jnp.bfloat16),
        query_mask.astype(jnp.bfloat16),
        key_mask.astype(jnp.bfloat16),
        own_q,
    )


def attend_kernel(q_ref, k_ref, v_ref, o_ref, lse_ref):
    queries, keys, values = q_ref[...], k_ref[...], v_ref[...]
    outs = []
    for head in range(2):
        _, query_mask, key_mask, own = head_operands(queries, keys, head)
        scores = dot(query_mask, key_mask, 1, 1)
        largest = jnp.max(scores, axis=-1, keepdims=True)
        expo = jnp.exp(scores - largest)
        totals = jnp.sum(expo, axis=-1, keepdims=True)
        outs.append(dot(expo.astype(jnp.bfloat16), values, 1, 0) / totals)
        logs = largest + jnp.log(totals)
        wide = jnp.transpose(jnp.broadcast_to(logs, (logs.shape[0], LANES)))
        lse_ref[pl.ds(head * 4, 4), :] = wide[:4]
    lane = lax.broadcasted_iota(jnp.int32, outs[0].shape, 1)
    o_ref[...] = jnp.where(lane < HD, outs[0], outs[1]).astype(o_ref.dtype)


def attend(joint, head_cols):
    seq_rows = joint.shape[0]
    pairs = head_cols // LANES
    block = seq_rows // Q_SPLIT
    cols = pl.BlockSpec((block, LANES), lambda p, i: (i, p))
    return pl.pallas_call(
        attend_kernel,
        name="attend",
        grid=(pairs, Q_SPLIT),
        in_specs=[
            cols,
            pl.BlockSpec((seq_rows, LANES), lambda p, i: (0, pairs + p)),
            pl.BlockSpec((seq_rows, LANES), lambda p, i: (0, 2 * pairs + p)),
        ],
        out_specs=[
            cols,
            pl.BlockSpec((None, None, 8, block), lambda p, i: (p, i, 0, 0)),
        ],
        out_shape=[
            jax.ShapeDtypeStruct((seq_rows, head_cols), jnp.bfloat16),
            jax.ShapeDtypeStruct((pairs, Q_SPLIT, 8, block), jnp.float32),
        ],
        compiler_params=pltpu.CompilerParams(vmem_limit_bytes=56 * 1024 * 1024),
        cost_estimate=pl.CostEstimate(
            flops=4 * seq_rows * seq_rows * head_cols * 4,
            bytes_accessed=8 * seq_rows * head_cols,
            transcendentals=seq_rows * seq_rows * head_cols // HD,
        ),
    )(joint, joint, joint)


def attend_back_kernel(
    q_ref, k_ref, v_ref, do_ref, lse_ref, dq_ref, dk_ref, dv_ref, qs_ref, vs_ref, dk_acc, dv_acc
):
    step = pl.program_id(1)

    @pl.when(step == 0)
    def _():
        dk_acc[...] = jnp.zeros_like(dk_acc)
        dv_acc[...] = jnp.zeros_like(dv_acc)
        qs_ref[...] = jnp.zeros_like(qs_ref)

    queries, keys, values, grads = q_ref[...], k_ref[...], v_ref[...], do_ref[...]
    parts = []
    for head in range(2):
        query_plain, query_mask, key_mask, own = head_operands(queries, keys, head)
        own_grads = jnp.where(own, grads.astype(jnp.float32), 0.0).astype(jnp.bfloat16)
        scores = dot(key_mask, query_mask, 1, 1)
        shares = jnp.exp(scores - lse_ref[head * 4 : head * 4 + 1, :])
        share_grad = dot(values, own_grads, 1, 1)
        inner = jnp.sum(shares * share_grad, axis=0, keepdims=True)
        score_grad = (shares * (share_grad - inner)).astype(jnp.bfloat16)
        dv_acc[...] += dot(shares.astype(jnp.bfloat16), own_grads, 1, 0)
        dk_acc[...] += dot(score_grad, query_plain, 1, 0)
        parts.append(dot(keys, score_grad, 0, 0))
    row = lax.broadcasted_iota(jnp.int32, parts[0].shape, 0)
    query_grad = jnp.transpose(jnp.where(row < HD, parts[0], parts[1])) * 0.125
    dq_ref[...] = query_grad.astype(dq_ref.dtype)
    qs_ref[...] += jnp.broadcast_to(jnp.sum(query_grad, axis=0, keepdims=True), qs_ref.shape)

    @pl.when(step == pl.num_programs(1) - 1)
    def _():
        dk_ref[...] = dk_acc[...].astype(dk_ref.dtype)
        dv_ref[...] = dv_acc[...].astype(dv_ref.dtype)
        vs_ref[...] = jnp.broadcast_to(
            jnp.sum(dv_acc[...], axis=0, keepdims=True), vs_ref.shape
        )


def attend_back(joint, grads, logs, head_cols):
    seq_rows = joint.shape[0]
    pairs = head_cols // LANES
    block = seq_rows // Q_SPLIT
    cols = pl.BlockSpec((block, LANES), lambda p, i: (i, p))
    whole = pl.BlockSpec((seq_rows, LANES), lambda p, i: (0, p))
    sums = pl.BlockSpec((8, LANES), lambda p, i: (0, p))
    return pl.pallas_call(
        attend_back_kernel,
        name="attend_back",
        grid=(pairs, Q_SPLIT),
        in_specs=[
            cols,
            pl.BlockSpec((seq_rows, LANES), lambda p, i: (0, pairs + p)),
            pl.BlockSpec((seq_rows, LANES), lambda p, i: (0, 2 * pairs + p)),
            cols,
            pl.BlockSpec((None, None, 8, block), lambda p, i: (p, i, 0, 0)),
        ],
        out_specs=[cols, whole, whole, sums, sums],
        out_shape=[jax.ShapeDtypeStruct((seq_rows, head_cols), jnp.bfloat16)] * 3
        + [jax.ShapeDtypeStruct((8, head_cols), jnp.float32)] * 2,
        scratch_shapes=[pltpu.VMEM((seq_rows, LANES), jnp.float32)] * 2,
        compiler_params=pltpu.CompilerParams(vmem_limit_bytes=56 * 1024 * 1024),
        cost_estimate=pl.CostEstimate(
            flops=10 * seq_rows * seq_rows * head_cols * 4,
            bytes_accessed=16 * seq_rows * head_cols,
            transcendentals=seq_rows * seq_rows * head_cols // HD,
        ),
    )(joint, joint, joint, grads, logs)


def body(
    tokens,
    w_query,
    w_key,
    w_value,
    w_out,
    w_up,
    w_down,
    norm1_gain,
    norm1_bias,
    query_bias,
    value_bias,
    out_bias,
    scale1,
    norm2_gain,
    norm2_bias,
    up_bias,
    down_bias,
    scale2,
    out_grad,
):
    image_count, shard_rows, width = tokens.shape
    tp_count = lax.axis_size("tp")
    tp_index = lax.axis_index("tp")
    local_rows = image_count * shard_rows
    head_cols = w_query.shape[1]
    hidden_cols = w_up.shape[1]
    hidden_all = hidden_cols * tp_count
    shard_width = w_up.shape[0]
    bf16 = jnp.bfloat16

    own_tokens = tokens.astype(jnp.float32)
    xhat1, inverse1 = layer_norm_parts(own_tokens)
    normed_own = (xhat1 * norm1_gain + norm1_bias).astype(bf16)
    w_joint = lax.all_gather(
        jnp.concatenate([w_query, w_key, w_value], axis=1), "fsdp", axis=0, tiled=True
    )
    normed = [
        lax.all_gather(normed_own[image], "tp", axis=0, tiled=True)
        for image in range(image_count)
    ]

    w_up_cols = lax.all_gather(w_up, "tp", axis=1, tiled=True)
    w_down_cols = lax.all_gather(w_down.T, "tp", axis=1, tiled=True)
    w_out_cols = lax.all_gather(w_out.T, "tp", axis=1, tiled=True)
    out_t = lax.all_gather(w_out_cols, "fsdp", axis=0, tiled=True)
    up = lax.all_gather(w_up_cols, "fsdp", axis=0, tiled=True)
    down_t = lax.all_gather(w_down_cols, "fsdp", axis=0, tiled=True)

    query_slice = lax.dynamic_slice_in_dim(query_bias, tp_index * head_cols, head_cols)
    value_slice = lax.dynamic_slice_in_dim(value_bias, tp_index * head_cols, head_cols)
    joint_bias = jnp.concatenate([query_slice, jnp.zeros((head_cols,), jnp.float32), value_slice])

    joints, logs, owned = [], [], []
    for image in range(image_count):
        joint = (dot(normed[image], w_joint, 1, 0) + joint_bias).astype(bf16)
        attended, log_totals = attend(joint, head_cols)
        joints.append(joint)
        logs.append(log_totals)
        owned.append(lax.all_to_all(attended, "tp", 0, 1, tiled=True))
    attended_own = jnp.concatenate(owned, axis=0)

    rows = own_tokens.reshape(local_rows, width)
    branch = dot(attended_own, out_t, 1, 1) + out_bias
    middle = rows + scale1 * branch
    xhat2, inverse2 = layer_norm_parts(middle)
    normed2 = (xhat2 * norm2_gain + norm2_bias).astype(bf16)
    preact = dot(normed2, up, 1, 0) + up_bias
    normal = 0.5 * (1.0 + lax.erf(preact * math.sqrt(0.5)))
    density = jnp.exp(-0.5 * preact * preact) * (1.0 / math.sqrt(2.0 * math.pi))
    hidden = (preact * normal).astype(bf16)
    slope = normal + preact * density
    feed = dot(hidden, down_t, 1, 1) + down_bias
    positions = tp_index * shard_rows + jnp.arange(shard_rows)
    row_valid = jnp.tile((positions < SEQ).astype(jnp.float32), image_count)[:, None]
    output = (row_valid * (middle + scale2 * feed)).astype(bf16).reshape(tokens.shape)

    grad_final = row_valid * out_grad.reshape(local_rows, width).astype(jnp.float32)
    scale2_part = jnp.sum(grad_final * feed, axis=0)
    grad_feed = scale2 * grad_final
    down_bias_part = jnp.sum(grad_feed, axis=0)
    feed_low = grad_feed.astype(bf16)
    down_grad = dot(feed_low, hidden, 0, 0).astype(bf16)
    down_grad = lax.psum_scatter(down_grad, "fsdp", scatter_dimension=0, tiled=True)
    pre_grad = dot(feed_low, down_t, 1, 0) * slope
    up_part = jnp.sum(pre_grad, axis=0)
    pre_low = pre_grad.astype(bf16)
    up_grad = dot(normed2, pre_low, 0, 0).astype(bf16)
    up_grad = lax.psum_scatter(up_grad, "fsdp", scatter_dimension=0, tiled=True)
    normed2_grad = dot(pre_low, up, 1, 1)
    middle_part, gain2_part, bias2_part = layer_norm_back(
        normed2_grad, xhat2, inverse2, norm2_gain
    )
    middle_grad = grad_final + middle_part
    scale1_part = jnp.sum(middle_grad * branch, axis=0)
    grad_branch = scale1 * middle_grad
    out_bias_part = jnp.sum(grad_branch, axis=0)
    branch_low = grad_branch.astype(bf16)
    attn_grad_own = dot(branch_low, out_t, 1, 0).astype(bf16)
    out_grad_t = dot(branch_low, attended_own, 0, 0).astype(bf16)
    out_grad_t = lax.psum_scatter(out_grad_t, "fsdp", scatter_dimension=0, tiled=True)

    joint_part = 0.0
    query_part = 0.0
    value_part = 0.0
    normed_grads = []
    for image in range(image_count):
        lower = image * shard_rows
        attn_grad = lax.all_to_all(
            attn_grad_own[lower : lower + shard_rows], "tp", 1, 0, tiled=True
        )
        dq, dk, dv, q_sums, v_sums = attend_back(joints[image], attn_grad, logs[image], head_cols)
        joint_low = jnp.concatenate([dq, dk, dv], axis=1)
        query_part = query_part + q_sums[0]
        value_part = value_part + v_sums[0]
        joint_part = joint_part + dot(normed[image], joint_low, 0, 0)
        partial = dot(joint_low, w_joint, 1, 1).astype(bf16)
        normed_grads.append(lax.psum_scatter(partial, "tp", scatter_dimension=0, tiled=True))
    joint_sum = lax.psum_scatter(
        joint_part.astype(bf16), "fsdp", scatter_dimension=0, tiled=True
    ).astype(jnp.float32)
    normed_grad = jnp.stack(normed_grads).astype(jnp.float32)
    input_part, gain1_part, bias1_part = layer_norm_back(normed_grad, xhat1, inverse1, norm1_gain)
    tokens_grad = middle_grad.reshape(tokens.shape) + input_part

    def own_columns(summed, count):
        return lax.psum_scatter(summed, "tp", scatter_dimension=1, tiled=True).astype(jnp.float32)

    w_up_grad = own_columns(up_grad, hidden_cols)
    w_down_grad = own_columns(down_grad, hidden_cols).T
    w_out_grad = own_columns(out_grad_t, head_cols).T

    def placed(part, like, count):
        return lax.dynamic_update_slice_in_dim(
            jnp.zeros_like(like), part, tp_index * count, 0
        )

    small = [
        gain1_part,
        bias1_part,
        placed(query_part, query_bias, head_cols),
        placed(value_part, value_bias, head_cols),
        out_bias_part,
        scale1_part,
        gain2_part,
        bias2_part,
        up_part,
        down_bias_part,
        scale2_part,
    ]
    sums = lax.psum(tuple(small), ("fsdp", "tp"))
    return (
        output,
        tokens_grad,
        joint_sum[:, :head_cols],
        joint_sum[:, head_cols : 2 * head_cols],
        joint_sum[:, 2 * head_cols :],
        w_out_grad,
        w_up_grad,
        w_down_grad,
        *sums,
    )


def solution(mesh):
    rows = P("fsdp", "tp", None)
    by_rows = P("fsdp", "tp")
    by_cols = P("tp", "fsdp")
    weights = (by_rows, by_rows, by_rows, by_cols, by_rows, by_cols)
    return jax.shard_map(
        body,
        mesh=mesh,
        in_specs=(rows, *weights, *([P()] * 11), rows),
        out_specs=(rows, rows, *weights, *([P()] * 11)),
        check_vma=False,
    )
```
